32 devices in a mesh: segment: 4 (over y, x), dp: 8 (over z, core).
Axes of the slice: x: 2, y: 2, z: 4, core: 2. Of those that a mesh axis runs over, the one named last changes fastest.
Arguments:
- frozen_in: bfloat16 [8, 8, 4, 32, 320], P('dp'), may hold values from -6 to 6
- control_in: bfloat16 [8, 8, 4, 32, 320], P('dp'), may hold values from -6 to 6
- cotangent: bfloat16 [8, 8, 4, 32, 320], P('dp'), may hold values from -6 to 6
- frozen_weight: bfloat16 [4, 2880, 320], P('segment', None, 'dp'), may hold values from -0.109375 to 0.109375
- control_weight: bfloat16 [4, 2880, 320], P('segment', None, 'dp'), may hold values from -0.109375 to 0.109375
- zero_weight: bfloat16 [4, 320, 320], P('segment', None, 'dp'), may hold values from -0.3125 to 0.3125
Outputs:
- grad_control: float32 [4, 2880, 320], P('segment', None, 'dp')
- grad_zero: float32 [4, 320, 320], P('segment', None, 'dp')
The draws below stay inside these ranges and needn't reach their ends.
All inputs are finite; a program needn't handle non-finite values.
Results may differ from the reference program's by a relative error of at most 0.035.
Values may be sent and summed in bfloat16 or wider, within the bound.
No kernel may reach another device: no remote copies, remote signals or barrier semaphores. Data moves between devices by JAX's collectives and lax.ppermute only.
A program may use at most 64 MiB of HBM per device.

```python
import math
import jax
import jax.numpy as jnp
from jax import lax

C = 320
LAT_H = 4
LAT_W = 32
MB = 8
SEGMENTS = 4
LANES = 8


def with_spikes(values, rng, source, target, blocks, factor):
    def block_of(axis_at):
        return (jnp.arange(values.shape[axis_at]) // (values.shape[axis_at] // blocks)).reshape((-1,) + (1,) * (values.ndim - 1 - axis_at))

    one_side = jax.random.permutation(rng, blocks)[block_of(target)]
    other_side = (block_of(target) + blocks // 2) % blocks
    return jnp.where((block_of(source) == one_side) | (block_of(source) == other_side), factor * values, values)


def block_scale(stream_key, shape, split, low, largest):
    def one(dim, shards_of):
        heights = jax.random.uniform(jax.random.fold_in(jax.random.fold_in(stream_key, 6), dim), (shards_of,), jnp.float32, low / len(split), largest / len(split))
        return jnp.repeat(jnp.exp(heights), shape[dim] // shards_of).reshape((-1,) + (1,) * (len(shape) - dim - 1))

    loudness = one(*split[0])
    for cut in split[1:]:
        loudness = loudness * one(*cut)
    return loudness


def centred(rng, dims, scale, bound, cuts=(), kind=jnp.bfloat16):
    array = jax.random.normal(rng, dims, jnp.float32) * scale
    if len(cuts) > 0:
        array = block_scale(rng, dims, cuts, -0.22, 0.18) * array
    return jnp.clip(array, min=-bound, max=bound).astype(kind)


def gaussian_with(stream_key, dims, deviation, reach, split, heavy, dtype=jnp.bfloat16):
    array = deviation * jax.random.normal(stream_key, dims, jnp.float32)
    if split:
        array = array * block_scale(stream_key, dims, split, -0.22, 0.18)
    return jnp.clip(with_spikes(array, jax.random.fold_in(stream_key, 3), *heavy), -reach, reach).astype(dtype)


def setup_inputs(seed: int = 0) -> dict:
    key_of = jax.random.split(jax.random.key(seed), 7)
    return {
        "frozen_in": centred(key_of[0], (LANES, MB, LAT_H, LAT_W, C), 1.0, 6.0, ((0, 8),)),
        "control_in": centred(key_of[1], (LANES, MB, LAT_H, LAT_W, C), 1.0, 6.0, ((0, 8),)),
        "cotangent": gaussian_with(key_of[2], (LANES, MB, LAT_H, LAT_W, C), 1.0, 6.0, ((0, 8),), (0, 4, 8, 2.0)),
        "frozen_weight": centred(key_of[3], (SEGMENTS, 9 * C, C), (9 * C) ** -0.5, 0.109375, ((0, 4), (2, 8))),
        "control_weight": centred(key_of[4], (SEGMENTS, 9 * C, C), (9 * C) ** -0.5, 0.109375, ((0, 4), (2, 8))),
        "zero_weight": centred(key_of[5], (SEGMENTS, C, C), C ** -0.5, 0.3125, ((0, 4), (2, 8))),
    }


def unfold(latent):
    lat_height = latent.shape[-3]
    lat_width = latent.shape[-2]
    padding = [(0, 0)] * (latent.ndim - 3) + [(1, 1), (1, 1), (0, 0)]
    padded = jnp.pad(latent, padding)
    pieces = [padded[..., row_off:row_off + lat_height, col_off:col_off + lat_width, :] for row_off in range(3) for col_off in range(3)]
    return jnp.concatenate(pieces, axis=-1)

def conv_three(latent, weight):
    columns = unfold(latent)
    flattened = columns.reshape(-1, columns.shape[-1])
    result = jnp.dot(flattened, weight, preferred_element_type=jnp.float32)
    return result.reshape(latent.shape[:-1] + (weight.shape[1],))

def flipped(weight):
    channels = weight.shape[1]
    blocks = weight.reshape(9, -1, channels)[::-1]
    return jnp.transpose(blocks, (0, 2, 1)).reshape(9 * channels, -1)

def filter_grad(latent, gradient):
    columns = unfold(latent)
    flattened = columns.reshape(-1, columns.shape[-1])
    return lax.dot_general(flattened, gradient.reshape(-1, gradient.shape[-1]), (((0,), (0,)), ((), ())), preferred_element_type=jnp.float32)

def silu_slope(values):
    sig_value = jax.nn.sigmoid(values)
    return sig_value * (1.0 + values * (1.0 - sig_value))

def lane_grads(frozen_lane, control_lane, cot_lane, frozen_weight, control_weight, zero_weight):
    stream = frozen_lane
    control = control_lane
    saved_fields = []
    for section in range(SEGMENTS):
        pre_control = conv_three(control, control_weight[section])
        control_next = (control.astype(jnp.float32) + jax.nn.silu(pre_control)).astype(jnp.bfloat16)
        pre_frozen = conv_three(stream, frozen_weight[section])
        injected = jnp.dot(control_next.reshape(-1, C), zero_weight[section], preferred_element_type=jnp.float32).reshape(stream.shape)
        stream = (stream.astype(jnp.float32) + jax.nn.silu(pre_frozen) + injected).astype(jnp.bfloat16)
        saved_fields.append((control, control_next, pre_control, pre_frozen))
        control = control_next
    grad_stream = cot_lane
    grad_stream_control = jnp.zeros_like(control_lane)
    control_grads = [None] * SEGMENTS
    zero_grads = [None] * SEGMENTS
    for section in reversed(range(SEGMENTS)):
        control_input, control_out, pre_control, pre_frozen = saved_fields[section]
        flat_grad = grad_stream.reshape(-1, C)
        zero_grads[section] = lax.dot_general(control_out.reshape(-1, C), flat_grad, (((0,), (0,)), ((), ())), preferred_element_type=jnp.float32)
        frozen_part = (grad_stream.astype(jnp.float32) * silu_slope(pre_frozen)).astype(jnp.bfloat16)
        next_stream = (grad_stream.astype(jnp.float32) + conv_three(frozen_part, flipped(frozen_weight[section]))).astype(jnp.bfloat16)
        back_zero = lax.dot_general(flat_grad, zero_weight[section], (((1,), (1,)), ((), ())), preferred_element_type=jnp.float32)
        total_control = grad_stream_control.astype(jnp.float32) + back_zero.reshape(grad_stream.shape)
        control_part = (total_control * silu_slope(pre_control)).astype(jnp.bfloat16)
        grad_stream_control = (total_control + conv_three(control_part, flipped(control_weight[section]))).astype(jnp.bfloat16)
        control_grads[section] = filter_grad(control_input, control_part)
        grad_stream = next_stream
    return (jnp.stack(control_grads), jnp.stack(zero_grads))

def reference(frozen_in, control_in, cotangent, frozen_weight, control_weight, zero_weight):

    def accumulate(totals, lane_data):
        grads = lane_grads(lane_data[0], lane_data[1], lane_data[2], frozen_weight, control_weight, zero_weight)
        return ((totals[0] + grads[0], totals[1] + grads[1]), None)
    initial = (jnp.zeros((SEGMENTS, 9 * C, C), jnp.float32), jnp.zeros((SEGMENTS, C, C), jnp.float32))
    totals, unused = lax.scan(accumulate, initial, (frozen_in, control_in, cotangent))
    factor = 1.0 / math.sqrt(LANES * MB * LAT_H * LAT_W)
    return (totals[0] * factor, totals[1] * factor)
```

```python
import functools
import math

import jax
import jax.numpy as jnp
from jax import lax
from jax.experimental import pallas as pl
from jax.experimental.pallas import tpu as pltpu
from jax.sharding import PartitionSpec as P

VMEM = pl.BlockSpec(memory_space=pltpu.VMEM)
SMEM = pl.BlockSpec(memory_space=pltpu.SMEM)
ANY = pl.BlockSpec(memory_space=pl.ANY)
BF16 = jnp.bfloat16
F32 = jnp.float32
LANE = 128


def tap_masks(height, width):
    cells = height * width
    cell = lax.broadcasted_iota(jnp.int32, (1, cells), 1)
    row = cell // width
    col = cell - row * width
    masks = []
    for tap in range(9):
        down, right = tap // 3 - 1, tap % 3 - 1
        inside = (row + down >= 0) & (row + down < height) & (col + right >= 0) & (col + right < width)
        masks.append((down * width + right, inside))
    return masks


def write_columns(cols_ref, field, masks, cells, start=0):
    channels = field.shape[0]
    for micro in range(field.shape[1] // cells):
        part = field[:, micro * cells : (micro + 1) * cells]
        for tap, (offset, inside) in enumerate(masks):
            moved = part if offset == 0 else pltpu.roll(part, (-offset) % cells, 1)
            moved = moved if offset == 0 else jnp.where(inside, moved, 0.0)
            cols_ref[
                tap * channels : (tap + 1) * channels,
                start + micro * cells : start + (micro + 1) * cells,
            ] = moved.astype(BF16)


def dot(a, b):
    return jnp.dot(a, b, preferred_element_type=F32)


def dot_nt(a, b):
    return lax.dot_general(a, b, (((1,), (1,)), ((), ())), preferred_element_type=F32)


def silu_parts(values):
    sig = jax.nn.sigmoid(values)
    return values * sig, sig * (1.0 + values * (1.0 - sig))


def flip_into(flip_ref, full_ref, extra):
    channels = full_ref.shape[0]
    for tap in range(9):
        block = full_ref[:, (8 - tap) * channels : (9 - tap) * channels]
        flip_ref[:, tap * channels : (tap + 1) * channels] = block.T
    if extra is not None:
        flip_ref[:, extra : extra + channels] = full_ref[:, extra : extra + channels].T


def join_kernel(chips, extra, place_ref, *refs):
    pieces, (full_ref, flip_ref, sem) = refs[:-3], refs[-3:]
    chip, core = place_ref[1], place_ref[2]
    half = len(pieces) // 2
    copies = []
    for side in range(2):
        parity = core if side == 0 else 1 - core
        back = 0
        for piece in pieces[side * half : (side + 1) * half]:
            size = piece.shape[1]
            for entry in range(piece.shape[0]):
                lane = lax.rem(chip - back + chips, chips) * 2 + parity
                target = full_ref.at[pl.ds(pl.multiple_of(lane * size, 8), size)]
                copies.append(pltpu.make_async_copy(piece.at[entry], target, sem.at[len(copies)]))
                back += 1
    for copy in copies:
        copy.start()
    for copy in copies:
        copy.wait()
    flip_into(flip_ref, full_ref, extra)


def fetch(place, section, sources, target, sem):
    for k, source in enumerate(sources):

        @pl.when(lax.bitwise_xor(place, k) == section)
        def _(source=source):
            pltpu.make_async_copy(source, target, sem).start()


def arrived(sources, target, sem):
    pltpu.make_async_copy(sources[0], target, sem).wait()


def control_kernel(height, width, sections, place_ref, c0_ref, *refs):
    w_refs, (fields_ref, pairs_ref, slope_ref, weights, cols, sem) = refs[:sections], refs[sections:]
    taps = cols.shape[0]
    place = place_ref[0]
    for s in range(sections):
        fetch(place, s, w_refs, weights.at[s], sem.at[s])
    masks = tap_masks(height, width)
    rounded = c0_ref[...]
    for s in range(sections):
        control = rounded.astype(F32)
        slot = lax.bitwise_xor(place, s)
        pairs_ref[slot, 0] = rounded
        write_columns(cols, control, masks, height * width)
        arrived(w_refs, weights.at[s], sem.at[s])
        value, slope = silu_parts(dot(weights[s, :, :taps], cols[...]))
        slope_ref[s] = slope
        rounded = (control + value).astype(BF16)
        fields_ref[s] = rounded
        pairs_ref[slot, 1] = rounded


def frozen_kernel(height, width, sections, extra, place_ref, x0_ref, fields_ref, *refs):
    w_refs, z_refs = refs[:sections], refs[sections : 2 * sections]
    slope_ref, weights, zeros, cols, sem = refs[2 * sections :]
    channels = x0_ref.shape[0]
    place = place_ref[0]
    z_parts = [z.at[:, pl.ds(extra, channels)] for z in z_refs]
    for s in range(sections):
        fetch(place, s, w_refs, weights.at[s], sem.at[0, s])
        fetch(place, s, z_parts, zeros.at[s], sem.at[1, s])
    masks = tap_masks(height, width)
    stream = x0_ref[...].astype(F32)
    for s in range(sections):
        write_columns(cols, stream, masks, height * width)
        arrived(w_refs, weights.at[s], sem.at[0, s])
        arrived(z_parts, zeros.at[s], sem.at[1, s])
        value, slope = silu_parts(dot(weights[s], cols[...]))
        slope_ref[s] = slope
        if s < sections - 1:
            stream = (stream + value + dot(zeros[s], fields_ref[s])).astype(BF16).astype(F32)


def back_kernel(height, width, sections, extra, flipped, place_ref, gx_ref, sa_ref, sb_ref, *refs):
    f_refs, c_refs = refs[:sections], refs[sections : 2 * sections]
    pairs_ref, frozen, control, zero0, cols, sem = refs[2 * sections : 2 * sections + 6]
    frozen_turn, control_turn = (None, None) if flipped else refs[2 * sections + 6 :]
    channels = gx_ref.shape[0]
    taps = cols.shape[0]
    place = place_ref[0]
    z_parts = [c.at[:, pl.ds(extra, channels)] for c in c_refs]
    for s in reversed(range(1, sections)):
        fetch(place, s, c_refs, control.at[s - 1], sem.at[1, s])
        fetch(place, s, f_refs, frozen.at[s - 1], sem.at[0, s])
    fetch(place, 0, z_parts, zero0, sem.at[1, 0])
    masks = tap_masks(height, width)
    gx = gx_ref[...]
    gc = None
    for s in reversed(range(sections)):
        if s > 0:
            arrived(c_refs, control.at[s - 1], sem.at[1, s])
            control_now = control.at[s - 1]
            if not flipped:
                flip_into(control_turn, control_now, extra)
                control_now = control_turn
            zero = control_now[:, extra : extra + channels]
        else:
            arrived(z_parts, zero0, sem.at[1, 0])
            zero = zero0[...] if flipped else zero0[...].T
        slot = lax.bitwise_xor(place, s)
        total = dot(zero, gx) if gc is None else gc.astype(F32) + dot(zero, gx)
        part = (total * sa_ref[s]).astype(BF16)
        pairs_ref[slot, 0] = part
        pairs_ref[slot, 1] = gx
        if s > 0:
            wide = gx.astype(F32)
            fpart = (wide * sb_ref[s]).astype(BF16)
            write_columns(cols, fpart.astype(F32), masks, height * width)
            arrived(f_refs, frozen.at[s - 1], sem.at[0, s])
            frozen_now = frozen.at[s - 1]
            if not flipped:
                flip_into(frozen_turn, frozen_now, None)
                frozen_now = frozen_turn
            gx = (wide + dot(frozen_now[...], cols[...])).astype(BF16)
            write_columns(cols, part.astype(F32), masks, height * width)
            gc = (total + dot(control_now[:, :taps], cols[...])).astype(BF16)


def columns_kernel(height, width, *refs):
    pairs, (cols_ref, outs_ref) = refs[:-2], refs[-2:]
    masks = tap_masks(height, width)
    for k, pair in enumerate(pairs):
        rows = pair.shape[-1]
        write_columns(cols_ref, pair[0].astype(F32), masks, height * width, k * rows)
        outs_ref[:, k * rows : (k + 1) * rows] = pair[1]


def grads_kernel(order_ref, cols_ref, outs_ref, *refs):
    blocks = order_ref.shape[0]
    sections = len(refs) - blocks - 1
    pairs, grads, wide = refs[:sections], refs[sections:-1], refs[-1]
    channels, rows = pairs[0].shape[1:]
    size = channels // blocks
    taps = cols_ref.shape[0]
    parts = []
    for which in range(2):
        for k, pair in enumerate(pairs):
            wide[:, k * rows : (k + 1) * rows] = pair[which].astype(F32)
        if blocks == 1:
            parts.append(wide[...].astype(BF16))
            continue
        ordered = [wide[pl.ds(pl.multiple_of(order_ref[b] * size, 8), size), :] for b in range(blocks)]
        parts.append(jnp.concatenate(ordered).astype(BF16))
    main = dot_nt(parts[0], cols_ref[...])
    zero = dot_nt(parts[1], outs_ref[...])
    for b, grad in enumerate(grads):
        grad[:, :taps] = main[b * size : (b + 1) * size].astype(BF16)
        grad[:, taps:] = zero[b * size : (b + 1) * size].astype(BF16)


def call(name, kernel, outs, specs, scratch, *args):
    size = sum(math.prod(a.shape) * a.dtype.itemsize for a in args)
    return pl.pallas_call(
        kernel,
        out_shape=outs,
        in_specs=specs,
        out_specs=jax.tree.map(lambda _: VMEM, outs),
        scratch_shapes=scratch,
        name=name,
        cost_estimate=pl.CostEstimate(flops=2 * 10**9, bytes_accessed=size, transcendentals=0),
        compiler_params=pltpu.CompilerParams(vmem_limit_bytes=60 * 2**20),
    )(*args)


def local(frozen_in, control_in, cotangent, frozen_weight, control_weight, zero_weight):
    segments = lax.axis_size("segment")
    lanes = lax.axis_size("dp")
    position = lax.axis_index("segment")
    lane = lax.axis_index("dp")
    _, micro_count, height, width, channels = frozen_in.shape
    size = frozen_weight.shape[2]
    share = micro_count // segments
    cells = height * width
    rows = share * cells
    taps = 9 * channels
    extra = -(-taps // LANE) * LANE
    chips = lanes // 2
    blocked = size % 8 == 0
    sds = jax.ShapeDtypeStruct
    place = jnp.stack([position, lane // 2, lane % 2]).astype(jnp.int32)

    def mine(array):
        part = lax.dynamic_slice_in_dim(array[0], position * share, share, 0)
        return part.reshape(rows, channels).T

    x0, c0, gx = mine(frozen_in), mine(control_in), mine(cotangent)
    control_rows = jnp.concatenate(
        [control_weight[0].T, jnp.zeros((size, extra - taps), BF16), zero_weight[0].T], axis=1
    )
    frozen_rows = frozen_weight[0].T

    def move_chip(x, by):
        return lax.ppermute(x, "dp", [(i, (i + 2 * by) % lanes) for i in range(lanes)])

    def move_core(x):
        return lax.ppermute(x, "dp", [(i, i ^ 1) for i in range(lanes)])

    def move_column(x, by):
        return lax.ppermute(x, "segment", [(i, i ^ by) for i in range(segments)])

    def spread(x, bits):
        have = {0: x}
        for bit in bits:
            have.update({k ^ bit: move_column(v, bit) for k, v in list(have.items())})
        return have

    def gathered(own, tail):
        if not blocked:
            full = lax.all_gather(own, "dp", axis=0, tiled=True)
            wholes = [full] + [move_column(full, k) for k in range(1, segments)]
            return [(whole, whole) for whole in wholes]
        near = [own] + [move_chip(own, by) for by in range(1, chips)]
        half = (chips + 1) // 2
        bits = [1 << i for i in range(segments.bit_length() - 1)]
        groups = [spread(jnp.stack(near[:half]), bits)]
        if chips > 1:
            groups.append(spread(jnp.stack(near[half:]), bits[::-1]))
        result = []
        for k in range(segments):
            kept = [group[k] for group in groups]
            pieces = kept + [move_core(piece) for piece in kept]
            shape = sds((channels, own.shape[1]), BF16)
            kernel = functools.partial(join_kernel, chips, tail)
            scratch = [pltpu.SemaphoreType.DMA((lanes,))]
            specs = [SMEM] + [ANY] * len(pieces)
            result.append(call("join", kernel, (shape, shape), specs, scratch, place, *pieces))
        return result

    control = gathered(control_rows, extra)
    fields, pairs, slope_a = call(
        "control",
        functools.partial(control_kernel, height, width, segments),
        (
            sds((segments, channels, rows), BF16),
            sds((segments, 2, channels, rows), BF16),
            sds((segments, channels, rows), F32),
        ),
        [SMEM, VMEM] + [ANY] * segments,
        [
            pltpu.VMEM((segments, channels, extra + channels), BF16),
            pltpu.VMEM((taps, rows), BF16),
            pltpu.SemaphoreType.DMA((segments,)),
        ],
        place,
        c0,
        *[full for full, _ in control],
    )
    field_pairs = [pairs[0]] + [move_column(pairs[k], k) for k in range(1, segments)]
    all_rows = segments * rows
    cols, outs = call(
        "columns",
        functools.partial(columns_kernel, height, width),
        (sds((taps, all_rows), BF16), sds((channels, all_rows), BF16)),
        [VMEM] * segments,
        [],
        *field_pairs,
    )
    frozen = gathered(frozen_rows, None)
    slope_b = call(
        "frozen",
        functools.partial(frozen_kernel, height, width, segments, extra),
        sds((segments, channels, rows), F32),
        [SMEM, VMEM, VMEM] + [ANY] * (2 * segments),
        [
            pltpu.VMEM((segments, channels, taps), BF16),
            pltpu.VMEM((segments, channels, channels), BF16),
            pltpu.VMEM((taps, rows), BF16),
            pltpu.SemaphoreType.DMA((2, segments)),
        ],
        place,
        x0,
        fields,
        *[full for full, _ in frozen],
        *[full for full, _ in control],
    )
    turns = [] if blocked else [pltpu.VMEM((channels, taps), BF16), pltpu.VMEM((channels, extra + channels), BF16)]
    parts = call(
        "back",
        functools.partial(back_kernel, height, width, segments, extra, blocked),
        sds((segments, 2, channels, rows), BF16),
        [SMEM, VMEM, VMEM, VMEM] + [ANY] * (2 * segments),
        [
            pltpu.VMEM((max(segments - 1, 1), channels, taps), BF16),
            pltpu.VMEM((max(segments - 1, 1), channels, extra + channels), BF16),
            pltpu.VMEM((channels, channels), BF16),
            pltpu.VMEM((taps, rows), BF16),
            pltpu.SemaphoreType.DMA((2, segments)),
        ]
        + turns,
        place,
        gx,
        slope_a,
        slope_b,
        *[flip for _, flip in frozen],
        *[flip for _, flip in control],
    )
    part_pairs = [parts[0]] + [move_column(parts[k], k) for k in range(1, segments)]
    blocks = lanes if blocked else 1
    if blocked:
        ahead = [(lane // 2 + by) % chips * 2 for by in range(chips)]
        order = jnp.stack([a + lane % 2 for a in ahead] + [a + 1 - lane % 2 for a in ahead]).astype(jnp.int32)
    else:
        order = jnp.zeros((1,), jnp.int32)
    grads = call(
        "grads",
        grads_kernel,
        (sds((channels // blocks, taps + channels), BF16),) * blocks,
        [SMEM] + [VMEM] * (2 + segments),
        [pltpu.VMEM((channels, all_rows), F32)],
        order,
        cols,
        outs,
        *part_pairs,
    )
    factor = 1.0 / math.sqrt(lanes * micro_count * cells)
    if blocked:
        sums = []
        for by in range(chips):
            sums.append(grads[by].astype(F32) + move_core(grads[chips + by]).astype(F32))
        total = sums[0]
        for by in range(1, chips):
            total = total + move_chip(sums[by].astype(BF16), by).astype(F32)
    else:
        total = lax.psum_scatter(grads[0], "dp", scatter_dimension=0, tiled=True).astype(F32)
    result = (total * factor).T
    return result[:taps][None], result[taps:][None]


def solution(mesh):
    return jax.shard_map(
        local,
        mesh=mesh,
        in_specs=(P("dp"), P("dp"), P("dp")) + (P("segment", None, "dp"),) * 3,
        out_specs=(P("segment", None, "dp"),) * 2,
        check_vma=False,
    )
```
